32 devices in a mesh: groups: 2 (over y), band: 4 (over z), wt: 4 (over x, core).
Axes of the slice: x: 2, y: 2, z: 4, core: 2. Of those that a mesh axis runs over, the one named last changes fastest.
Arguments:
- prior_state: float32 [128, 16, 1024], P('groups', 'band', 'wt'), parts along dimension 0, may hold values from -6 to 6
- langevin_noise: float32 [4, 128, 16, 1024], P(None, 'groups', 'band', 'wt'), parts along dimension 1, may hold values from -6 to 6
- station_values: float32 [8192], P(('groups', 'band', 'wt')), parts along dimension 0, may hold values from -6 to 6
- entry_cell: int32 [8192], P(('groups', 'band', 'wt')), parts along dimension 0, may hold values from 0 to 65535
- entry_owner: int32 [8192], P(('groups', 'band', 'wt')), parts along dimension 0, may hold values from 0 to 3, as said below
- entry_slot: int32 [8192], P(('groups', 'band', 'wt')), parts along dimension 0, may hold values from 0 to 255
- entry_weight: float32 [8192], P(('groups', 'band', 'wt')), parts along dimension 0, may hold values from 0.25 to 1
- live_counts: int32 [32], P(('groups', 'band', 'wt')), parts along dimension 0, may hold values from 64 to 256, as said below
- lift_weight: bfloat16 [64, 256], replicated, may hold values from -0.75 to 0.75
- conv_weight: bfloat16 [9, 256, 256], replicated, may hold values from -0.125 to 0.125
- head_weight: bfloat16 [256, 64], replicated, may hold values from -0.375 to 0.375
- first_gain: float32 [256], replicated, may hold values from 0.1 to 1.9
- second_gain: float32 [256], replicated, may hold values from 0.1 to 1.9
Outputs:
- analysis_state: float32 [128, 16, 1024], P('groups', 'band', 'wt'), parts along dimension 0
- innovation: float32 [8192], P(('groups', 'band', 'wt')), parts along dimension 0
The draws below stay inside these ranges and needn't reach their ends.
There are 2 independent parts, one for each index of `groups`. The reference program is written for one: setup_inputs(seed, part) draws one part's arguments, and reference() takes and returns one part's arrays. A program takes and returns all parts, laid end to end along the dimension named above; an argument that names none is the same for every part. Nothing has to cross between parts.
Inputs may be any that keep to these rules, and one draw needn't show every extreme that they name: `entry_owner`: an entry's owner band lies within 2 bands of the entry's own band; every list holds an entry at offset +2 and one at -2, clipped to the existing bands. `live_counts`: some list is full in every draw.
All inputs are finite; a program needn't handle non-finite values.
Results may differ from the reference program's by a relative error of at most 0.0014.
Values may be sent and summed in bfloat16 or wider, within the bound.
A program may use at most 64 MiB of HBM per device.

```python
import math
import jax
import jax.numpy as jnp
from jax import lax

VARS = 64
CHAN = 256
LATB = 4
LOND = 256
S_DEV = 256
ENT = 256
REACH = 2
NLAT = 16
NLON = 1024
NSTAT = 4096
ENTRIES = 4096
N_BAND = 4
N_WT = 4


def draw_entry_owner(key, part):
    total = ENT * N_BAND * N_WT
    position = jnp.arange(total, dtype=jnp.int32)
    band_of = position // ENT // N_WT
    offset = jax.random.randint(jax.random.fold_in(key, 11), (total,), -REACH, REACH + 1)
    within = position % ENT
    offset = jnp.where(within == 0, REACH, jnp.where(within == 1, -REACH, offset))
    return jnp.clip(band_of + offset, 0, N_BAND - 1).astype(jnp.int32)


def draw_live_counts(key, part):
    lists = N_BAND * N_WT
    counts = jax.random.randint(jax.random.fold_in(key, 21), (lists,), ENT // 4, ENT + 1)
    fullest = jax.random.randint(jax.random.fold_in(key, 22), (), 0, lists)
    return jnp.where(jnp.arange(lists, dtype=jnp.int32) == fullest, ENT, counts).astype(jnp.int32)


def place_ends(values, own_key, low, top_value):
    dims = values.shape
    index_at = [jax.random.randint(jax.random.fold_in(own_key, axis), (), 0, dims[axis]) for axis in range(len(dims))]
    values = values.at[tuple(index_at)].set(low)
    longest = dims.index(max(dims))
    index_at[longest] = (index_at[longest] + 1) % dims[longest]
    return values.at[tuple(index_at)].set(top_value)


def levels(key, extent, shards, low, high):
    level = 1.0
    for dim, blocks in shards:
        heights = jax.random.uniform(jax.random.fold_in(jax.random.fold_in(key, 6), dim), (blocks,), jnp.float32, low / len(shards), high / len(shards))
        level = level * jnp.repeat(jnp.exp(heights), extent[dim] // blocks).reshape((-1,) + (1,) * (len(extent) - 1 - dim))
    return level


def noise(own_key, extent, width, bound, split=(), kind=jnp.bfloat16):
    drawn = width * jax.random.normal(own_key, extent, jnp.float32)
    if split:
        drawn = drawn * levels(own_key, extent, split, -0.22, 0.18)
    return jnp.clip(drawn, -bound, bound).astype(kind)


def setup_inputs(seed: int = 0, part: int = 0) -> dict:
    streams_of = jax.random.split(jax.random.key(seed), 14)
    own_keys = jax.random.split(jax.random.fold_in(streams_of[13], part), 14)
    return {
        "prior_state": noise(own_keys[0], (VARS, NLAT, NLON), 1.0, 6.0, ((1, 4), (2, 4)), jnp.float32),
        "langevin_noise": noise(own_keys[1], (4, VARS, NLAT, NLON), 1.0, 6.0, ((2, 4), (3, 4)), jnp.float32),
        "station_values": noise(own_keys[2], (NSTAT,), 1.0, 6.0, ((0, 16),), jnp.float32),
        "entry_cell": place_ends(jax.random.randint(own_keys[3], (ENTRIES,), 0, VARS * LATB * LOND), jax.random.fold_in(own_keys[3], 1), 0, (VARS * LATB * LOND) - 1).astype(jnp.int32),
        "entry_owner": draw_entry_owner(jax.random.fold_in(jax.random.fold_in(streams_of[13], part), 71), part),
        "entry_slot": place_ends(jax.random.randint(own_keys[5], (ENTRIES,), 0, S_DEV), jax.random.fold_in(own_keys[5], 1), 0, S_DEV - 1).astype(jnp.int32),
        "entry_weight": jnp.clip(0.25 + 0.75 * jax.random.uniform(own_keys[6], (ENTRIES,), jnp.float32) ** levels(own_keys[6], (ENTRIES,), ((0, 16),), -0.2, 0.2), 0.25, 1.0),
        "live_counts": draw_live_counts(jax.random.fold_in(jax.random.fold_in(streams_of[13], part), 71), part),
        "lift_weight": noise(streams_of[8], (VARS, CHAN), VARS ** -0.5, 0.75),
        "conv_weight": noise(streams_of[9], (9, CHAN, CHAN), (9 * CHAN) ** -0.5, 0.125),
        "head_weight": noise(streams_of[10], (CHAN, VARS), CHAN ** -0.5, 0.375),
        "first_gain": jnp.clip(1.0 + 0.18 * jax.random.normal(streams_of[11], (CHAN,), jnp.float32), 0.1, 1.9),
        "second_gain": jnp.clip(1.0 + 0.18 * jax.random.normal(streams_of[12], (CHAN,), jnp.float32), 0.1, 1.9),
    }


noise_levels = (1.0, 0.6, 0.3)
obs_precision = 4.0
step_factor = 0.1

def rms_scale(values, gain):
    power = lax.optimization_barrier(jnp.mean(values * values, axis=0, keepdims=True))
    return values * lax.rsqrt(power + 1e-06) * gain[:, None, None]

def conv_global(hidden, conv_weight):
    padded = jnp.pad(hidden, ((0, 0), (1, 1), (0, 0)))
    padded = jnp.concatenate([padded[:, :, -1:], padded, padded[:, :, :1]], axis=2)
    total = jnp.zeros((conv_weight.shape[2], NLAT, NLON), jnp.float32)
    for tap_index in range(9):
        row_shift, col_shift = divmod(tap_index, 3)
        window = padded[:, row_shift:row_shift + NLAT, col_shift:col_shift + NLON].astype(jnp.float32)
        total = total + jnp.einsum('co,chw->ohw', conv_weight[tap_index].astype(jnp.float32), window)
    return total

def reference(prior_state, langevin_noise, station_values, entry_cell, entry_owner, entry_slot, entry_weight, live_counts, lift_weight, conv_weight, head_weight, first_gain, second_gain):
    position = jnp.arange(ENTRIES, dtype=jnp.int32)
    listed = position // ENT
    band_of = listed // N_WT
    sector = listed % N_WT
    alive = position % ENT < live_counts[listed]
    weights = jnp.where(alive, entry_weight, jnp.float32(0.0))
    variable = entry_cell // (LATB * LOND)
    remain = entry_cell % (LATB * LOND)
    rowpos = band_of * LATB + remain // LOND
    colpos = sector * LOND + remain % LOND
    flat_cell = (variable * NLAT * NLON + rowpos * NLON + colpos).astype(jnp.int32)
    station = ((entry_owner * N_WT + sector) * S_DEV + entry_slot).astype(jnp.int32)

    def evaluate(current, level):
        scaled = (current / math.sqrt(1.0 + level * level)).astype(jnp.bfloat16)
        lifted = jnp.einsum('vo,vhw->ohw', lift_weight.astype(jnp.float32), scaled.astype(jnp.float32))
        first = jax.nn.silu(rms_scale(lifted, first_gain)).astype(jnp.bfloat16)
        mixed = lifted + conv_global(first, conv_weight)
        second = jax.nn.silu(rms_scale(mixed, second_gain)).astype(jnp.bfloat16)
        score = jnp.einsum('co,chw->ohw', head_weight.astype(jnp.float32), second.astype(jnp.float32)) / level
        values = weights * current.reshape(-1)[flat_cell]
        interp = jnp.zeros((NSTAT,), jnp.float32).at[station].add(values)
        innov = station_values - interp
        adjoint = jnp.zeros((VARS * NLAT * NLON,), jnp.float32).at[flat_cell].add(weights * innov[station])
        return (score + obs_precision * adjoint.reshape(current.shape), innov)
    current = prior_state
    innov = station_values
    for section in range(2):
        upper = noise_levels[section]
        lower = noise_levels[section + 1]
        spread = upper * upper - lower * lower
        drift, innov = evaluate(current, upper)
        current = current + spread * drift + math.sqrt(spread) * langevin_noise[2 * section]
        factor = step_factor * lower * lower
        drift, innov = evaluate(current, lower)
        current = current + factor * drift + math.sqrt(2.0 * factor) * langevin_noise[2 * section + 1]
    return (current, innov)
```

```python
import functools
import math

import jax
import jax.numpy as jnp
from jax import lax
from jax.experimental import pallas as pl
from jax.experimental.pallas import tpu as pltpu
from jax.sharding import PartitionSpec as P

REACH = 2
SPAN = 2 * REACH
noise_levels = (1.0, 0.6, 0.3)
obs_precision = 4.0
step_factor = 0.1

F32 = jnp.float32
BF16 = jnp.bfloat16


def step_table():
    rows = []
    for section in range(2):
        upper = noise_levels[section]
        lower = noise_levels[section + 1]
        spread = upper * upper - lower * lower
        rows.append((upper, spread, math.sqrt(spread)))
        factor = step_factor * lower * lower
        rows.append((lower, factor, math.sqrt(2.0 * factor)))
    return rows


def choose(k, values):
    picked = F32(values[-1])
    for i in range(len(values) - 1):
        picked = jnp.where(k == i, F32(values[i]), picked)
    return picked


def nn(a, b):
    return lax.dot_general(a, b, (((1,), (0,)), ((), ())), preferred_element_type=F32)


def nt(a, b):
    return lax.dot_general(a, b, (((1,), (1,)), ((), ())), preferred_element_type=F32)


def halves(a):
    high = a.astype(BF16)
    low = (a - high.astype(F32)).astype(BF16)
    return high, low


def silu_rms(values, half_gain):
    power = jnp.mean(values * values, axis=0, keepdims=True)
    h = values * lax.rsqrt(power + 1e-06) * half_gain
    return h + h * jnp.tanh(h)


def kernel(
    nb, nw, rows, nv, nc, lon,
    x0, noise, sv, cell, owner, slot, weight, live, lift, conv, head, g1, g2,
    out, innov,
    x, sc, lifted, act, onehot, slothot, wmask, offmask,
    tsend, psend, rowbuf, tilebuf, partbuf,
    send_sem, recv_sem,
):
    me = lax.axis_index("band")
    col = lax.axis_index("wt")
    left = lax.rem(col + nw - 1, nw)
    right = lax.rem(col + 1, nw)
    dists = [d for d in range(-SPAN, SPAN + 1) if d != 0 and abs(d) < nb]

    def exists(d):
        return jnp.logical_and(me + d >= 0, me + d < nb)

    rowbuf[...] = jnp.zeros_like(rowbuf)
    tilebuf[...] = jnp.zeros_like(tilebuf)
    partbuf[...] = jnp.zeros_like(partbuf)

    barrier = pltpu.get_barrier_semaphore()

    def greet(b, w):
        pl.semaphore_signal(
            barrier, inc=1, device_id={"band": b, "wt": w}, device_id_type=pl.DeviceIdType.MESH
        )

    greet(me, left)
    greet(me, right)
    for d in dists:
        @pl.when(exists(d))
        def _():
            greet(me + d, col)
            if abs(d) == 1:
                greet(me + d, left)
                greet(me + d, right)

    e = cell.shape[1]
    c = cell[...]
    alive = lax.broadcasted_iota(jnp.int32, (1, e), 1) < live[0]
    weights = jnp.where(alive, weight[...], F32(0.0))
    var = c // (rows * lon)
    rest = c - var * (rows * lon)
    rowof = rest // lon
    lonof = rest - rowof * lon
    target = rowof * nv + var
    first_iota = lax.broadcasted_iota(jnp.int32, (lon, e), 0)
    onehot[...] = jnp.where(first_iota == lonof, F32(1.0), F32(0.0)).astype(BF16)
    slothot[...] = jnp.where(
        lax.broadcasted_iota(jnp.int32, (sv.shape[1], e), 0) == slot[...], F32(1.0), F32(0.0)
    ).astype(BF16)
    wmask[...] = jnp.where(
        lax.broadcasted_iota(jnp.int32, (rows * nv, e), 0) == target, weights, F32(0.0)
    )
    offset = owner[...] - me + REACH
    offmask[...] = jnp.where(
        lax.broadcasted_iota(jnp.int32, (8, e), 0) == offset, F32(1.0), F32(0.0)
    )
    x[...] = x0[...]

    peers = 2
    for d in dists:
        peers = peers + jnp.where(exists(d), 3 if abs(d) == 1 else 1, 0)
    pl.semaphore_wait(barrier, peers)

    lane = lax.broadcasted_iota(jnp.int32, (1, 128), 1)
    row8 = lax.broadcasted_iota(jnp.int32, (8, 1), 0)
    table = step_table()

    def step(k, carry):
        inverse = choose(k, [1.0 / math.sqrt(1.0 + r[0] * r[0]) for r in table])
        score_factor = choose(k, [r[1] / r[0] for r in table])
        adjoint_factor = choose(k, [obs_precision * r[1] for r in table])
        noise_factor = choose(k, [r[2] for r in table])

        def remote(index, source, target_ref, b, w):
            return pltpu.make_async_remote_copy(
                src_ref=source, dst_ref=target_ref,
                send_sem=send_sem.at[index], recv_sem=recv_sem.at[k, index],
                device_id={"band": b, "wt": w}, device_id_type=pl.DeviceIdType.MESH,
            )

        copies = [
            (None, remote(0, tsend, tilebuf.at[k, 0], me, right)),
            (None, remote(1, tsend, tilebuf.at[k, 1], me, left)),
            (1, remote(2, sc.at[rows - 1], rowbuf.at[k, 0], me + 1, col)),
            (-1, remote(3, sc.at[0], rowbuf.at[k, 1], me - 1, col)),
            (1, remote(4, tsend, tilebuf.at[k, 2], me + 1, right)),
            (1, remote(5, tsend, tilebuf.at[k, 3], me + 1, left)),
            (-1, remote(6, tsend, tilebuf.at[k, 4], me - 1, right)),
            (-1, remote(7, tsend, tilebuf.at[k, 5], me - 1, left)),
        ]
        parts = [
            (d, remote(8 + i, psend, partbuf.at[k, SPAN - d], me + d, col))
            for i, d in enumerate(dists)
        ]

        def when(d, f):
            if d is None:
                f()
            else:
                pl.when(exists(d))(f)

        tile = jnp.zeros((nv, 128), F32)
        for r in range(rows):
            s = x[pl.ds(r * nv, nv), :] * inverse
            sc[r] = s.astype(BF16)
            tail = pltpu.roll(s[:, lon - 128:], 2 * r + 3, 1)
            start = pltpu.roll(s[:, :128], 2 * r + 1, 1)
            tile = jnp.where(lane == 2 * r + 2, tail, tile)
            tile = jnp.where(lane == 2 * r + 1, start, tile)
        tsend[...] = tile.astype(BF16)
        for d, copy in copies:
            when(d, copy.start)

        high, low = halves(x[...])
        hot = onehot[...]
        picked = nn(high, hot) + nn(low, hot)
        values = jnp.sum(picked * wmask[...], axis=0, keepdims=True)
        high, low = halves(values * offmask[...])
        part = nt(high, slothot[...]) + nt(low, slothot[...])
        psend[...] = jnp.where(row8 == 2 * REACH + 1, sv[...], part)
        for d, copy in parts:
            when(d, copy.start)

        def widen(r, f):
            act[r, 1] = f.astype(BF16)
            near, far = f[:, :128], f[:, lon - 128:]
            a0, a1 = pltpu.roll(near, 1, 1), pltpu.roll(far, 1, 1)
            b0, b1 = pltpu.roll(near, 127, 1), pltpu.roll(far, 127, 1)
            act[r, 0, :, :128] = a0.astype(BF16)
            act[r, 0, :, 128:] = jnp.where(lane == 0, a0, a1).astype(BF16)
            act[r, 2, :, :128] = jnp.where(lane == 127, b1, b0).astype(BF16)
            act[r, 2, :, 128:] = b1.astype(BF16)

        half1 = g1[...]
        wide1 = jnp.concatenate([half1, half1], axis=1)
        for r in range(rows):
            v = nn(lift[...], sc[r])
            lifted[r] = v
            widen(r + 1, silu_rms(v, wide1))

        for d, copy in copies:
            when(None if d is None else -d, copy.wait_recv)
        for r, i in ((0, 0), (rows + 1, 1)):
            widen(r, silu_rms(nn(lift[...], rowbuf[k, i]), wide1))
        t = [tilebuf[k, i].astype(F32) for i in range(6)]
        edge = jnp.where(lane == 0, pltpu.roll(t[2], 128 - 2 * rows, 1), F32(0.0))
        edge = jnp.where(lane == 127, pltpu.roll(t[3], 128 - 2 * rows, 1), edge)
        inner = jnp.logical_and(lane >= 1, lane <= 2 * rows)
        even = lane % 2 == 0
        edge = jnp.where(jnp.logical_and(inner, even), t[0], edge)
        edge = jnp.where(jnp.logical_and(inner, jnp.logical_not(even)), t[1], edge)
        edge = jnp.where(lane == 2 * rows + 2, pltpu.roll(t[4], 2 * rows, 1), edge)
        edge = jnp.where(lane == 2 * rows + 1, pltpu.roll(t[5], 2 * rows, 1), edge)
        rim = silu_rms(nn(lift[...], edge.astype(BF16)), half1)
        for r in range(rows + 2):
            here = rim if r == 0 else pltpu.roll(rim, 128 - 2 * r, 1)
            now = act[r, 0, :, :128].astype(F32)
            act[r, 0, :, :128] = jnp.where(lane == 0, here, now).astype(BF16)
            now = act[r, 2, :, 128:].astype(F32)
            act[r, 2, :, 128:] = jnp.where(lane == 127, here, now).astype(BF16)

        half2 = g2[...]
        wide2 = jnp.concatenate([half2, half2], axis=1)
        scores = []
        for r in range(rows):
            window = act[pl.ds(r, 3)].reshape(9 * nc, lon)
            mixed = lifted[r] + nn(conv[...], window)
            second = silu_rms(mixed, wide2).astype(BF16)
            scores.append(nn(head[...], second))

        for d, copy in parts:
            when(-d, copy.wait_recv)
        mine = psend[...]
        total = mine
        observed = jnp.where(row8 == REACH, sv[...], F32(0.0))
        for d in dists:
            got = partbuf[k, d + SPAN]
            keep = jnp.logical_and(row8 >= max(0, d), row8 <= min(SPAN, SPAN + d))
            total = total + jnp.where(keep, pltpu.roll(got, d % 8, 0), F32(0.0))
            if abs(d) <= REACH:
                observed = jnp.where(row8 == d + REACH, got[SPAN + 1:SPAN + 2], observed)
        difference = jnp.where(row8 <= SPAN, observed - total, F32(0.0))
        innov[...] = difference[REACH:REACH + 1]
        high, low = halves(difference)
        back = nn(high, slothot[...]) + nn(low, slothot[...])
        back = jnp.sum(back * offmask[...], axis=0, keepdims=True)
        high, low = halves(wmask[...] * back)
        adjoint = nt(high, hot) + nt(low, hot)

        for r in range(rows):
            here = pl.ds(r * nv, nv)
            x[here, :] = (
                x[here, :]
                + score_factor * scores[r]
                + adjoint_factor * adjoint[r * nv:(r + 1) * nv]
                + noise_factor * noise[k, r * nv:(r + 1) * nv, :]
            )
        for d, copy in copies + parts:
            when(d, copy.wait_send)
        return carry

    lax.fori_loop(0, len(table), step, 0)
    out[...] = x[...]


def per_device(
    nb, nw,
    prior_state, langevin_noise, station_values, entry_cell, entry_owner, entry_slot,
    entry_weight, live_counts, lift_weight, conv_weight, head_weight, first_gain, second_gain,
):
    nv, rows, lon = prior_state.shape
    nc = lift_weight.shape[1]
    steps = langevin_noise.shape[0]
    stations = station_values.shape[0]
    e = entry_cell.shape[0]
    x0 = prior_state.transpose(1, 0, 2).reshape(rows * nv, lon)
    noise = langevin_noise.transpose(0, 2, 1, 3).reshape(steps, rows * nv, lon)
    conv = conv_weight.reshape(9 * nc, nc).T
    row = lambda a: a.reshape(1, -1)
    gain = lambda g: jnp.broadcast_to((0.5 * g)[:, None], (nc, 128))
    vmem = pl.BlockSpec(memory_space=pltpu.VMEM)
    count = 8 + 2 * SPAN
    state, innov = pl.pallas_call(
        functools.partial(kernel, nb, nw, rows, nv, nc, lon),
        out_shape=(
            jax.ShapeDtypeStruct((rows * nv, lon), F32),
            jax.ShapeDtypeStruct((1, stations), F32),
        ),
        in_specs=[vmem] * 7 + [pl.BlockSpec(memory_space=pltpu.SMEM)] + [vmem] * 5,
        out_specs=(vmem, vmem),
        scratch_shapes=[
            pltpu.VMEM((rows * nv, lon), F32),
            pltpu.VMEM((rows, nv, lon), BF16),
            pltpu.VMEM((rows, nc, lon), F32),
            pltpu.VMEM((rows + 2, 3, nc, lon), BF16),
            pltpu.VMEM((lon, e), BF16),
            pltpu.VMEM((stations, e), BF16),
            pltpu.VMEM((rows * nv, e), F32),
            pltpu.VMEM((8, e), F32),
            pltpu.VMEM((nv, 128), BF16),
            pltpu.VMEM((8, stations), F32),
            pltpu.VMEM((steps, 2, nv, lon), BF16),
            pltpu.VMEM((steps, 6, nv, 128), BF16),
            pltpu.VMEM((steps, 2 * SPAN + 1, 8, stations), F32),
            pltpu.SemaphoreType.DMA((count,)),
            pltpu.SemaphoreType.DMA((steps, count)),
        ],
        compiler_params=pltpu.CompilerParams(
            collective_id=0, has_side_effects=True, vmem_limit_bytes=40 * 1024 * 1024
        ),
    )(
        x0, noise, row(station_values), row(entry_cell), row(entry_owner), row(entry_slot),
        row(entry_weight), live_counts, lift_weight.T, conv, head_weight.T,
        gain(first_gain), gain(second_gain),
    )
    return state.reshape(rows, nv, lon).transpose(1, 0, 2), innov.reshape(-1)


def solution(mesh):
    ring = ("groups", "band", "wt")
    in_specs = (
        P(*ring), P(None, *ring), P(ring), P(ring), P(ring), P(ring), P(ring), P(ring),
        P(), P(), P(), P(), P(),
    )
    out_specs = (P(*ring), P(ring))
    return jax.shard_map(
        functools.partial(per_device, mesh.shape["band"], mesh.shape["wt"]),
        mesh=mesh, in_specs=in_specs, out_specs=out_specs, check_vma=False,
    )
```

```python
import functools
import math

import jax
import jax.numpy as jnp
from jax import lax
from jax.experimental import pallas as pl
from jax.experimental.pallas import tpu as pltpu
from jax.sharding import PartitionSpec as P

REACH = 2
SPAN = 2 * REACH
noise_levels = (1.0, 0.6, 0.3)
obs_precision = 4.0
step_factor = 0.1

F32 = jnp.float32
BF16 = jnp.bfloat16


def step_table():
    rows = []
    for section in range(2):
        upper = noise_levels[section]
        lower = noise_levels[section + 1]
        spread = upper * upper - lower * lower
        rows.append((upper, spread, math.sqrt(spread)))
        factor = step_factor * lower * lower
        rows.append((lower, factor, math.sqrt(2.0 * factor)))
    return rows


def choose(k, values):
    picked = F32(values[-1])
    for i in range(len(values) - 1):
        picked = jnp.where(k == i, F32(values[i]), picked)
    return picked


def nn(a, b):
    return lax.dot_general(a, b, (((1,), (0,)), ((), ())), preferred_element_type=F32)


def nt(a, b):
    return lax.dot_general(a, b, (((1,), (1,)), ((), ())), preferred_element_type=F32)


def halves(a):
    high = a.astype(BF16)
    low = (a - high.astype(F32)).astype(BF16)
    return high, low


def silu_rms(values, half_gain):
    power = jnp.mean(values * values, axis=0, keepdims=True)
    h = values * lax.rsqrt(power + 1e-06) * half_gain
    return h + h * jnp.tanh(h)


def kernel(
    nb, nw, rows, nv, nc, lon,
    x0, noise, sv, cell, owner, slot, weight, live, lift_in, conv_in, head, gain1, gain2,
    out, innov,
    x, lift, conv, g1, g2, sc, lifted, act, onehot, slothot, wmask, offmask,
    tsend, psend, rowbuf, tilebuf, partbuf,
    send_sem, recv_sem,
):
    me = lax.axis_index("band")
    col = lax.axis_index("wt")
    left = lax.rem(col + nw - 1, nw)
    right = lax.rem(col + 1, nw)
    sides = lon // 128

    def lines_of(r, h):
        return pl.ds(h * rows + r, nv, stride=sides * rows)

    dists = [d for d in range(-SPAN, SPAN + 1) if d != 0 and abs(d) < nb]

    def exists(d):
        return jnp.logical_and(me + d >= 0, me + d < nb)

    rowbuf[...] = jnp.zeros_like(rowbuf)
    tilebuf[...] = jnp.zeros_like(tilebuf)
    partbuf[...] = jnp.zeros_like(partbuf)

    barrier = pltpu.get_barrier_semaphore()

    def greet(b, w):
        pl.semaphore_signal(
            barrier, inc=1, device_id={"band": b, "wt": w}, device_id_type=pl.DeviceIdType.MESH
        )

    greet(me, left)
    greet(me, right)
    for d in dists:
        @pl.when(exists(d))
        def _():
            greet(me + d, col)
            if abs(d) == 1:
                greet(me + d, left)
                greet(me + d, right)

    e = cell.shape[1]
    c = cell[...]
    alive = lax.broadcasted_iota(jnp.int32, (1, e), 1) < live[0]
    weights = jnp.where(alive, weight[...], F32(0.0))
    var = c // (rows * lon)
    rest = c - var * (rows * lon)
    rowof = rest // lon
    lonof = rest - rowof * lon
    target = rowof * nv + var
    first_iota = lax.broadcasted_iota(jnp.int32, (lon, e), 0)
    onehot[...] = jnp.where(first_iota == lonof, F32(1.0), F32(0.0)).astype(BF16)
    slothot[...] = jnp.where(
        lax.broadcasted_iota(jnp.int32, (sv.shape[1], e), 0) == slot[...], F32(1.0), F32(0.0)
    ).astype(BF16)
    wmask[...] = jnp.where(
        lax.broadcasted_iota(jnp.int32, (rows * nv, e), 0) == target, weights, F32(0.0)
    )
    offset = owner[...] - me + REACH
    offmask[...] = jnp.where(
        lax.broadcasted_iota(jnp.int32, (8, e), 0) == offset, F32(1.0), F32(0.0)
    )
    for r in range(rows):
        for h in range(sides):
            x[pl.ds(r * nv, nv), 128 * h:128 * (h + 1)] = x0[lines_of(r, h), :]

    lift[...] = lift_in[...].T
    for t in range(9):
        conv[:, t * nc:(t + 1) * nc] = conv_in[t].T
    g1[...] = jnp.broadcast_to(0.5 * gain1[...], (128, nc)).T
    g2[...] = jnp.broadcast_to(0.5 * gain2[...], (128, nc)).T

    peers = 2
    for d in dists:
        peers = peers + jnp.where(exists(d), 3 if abs(d) == 1 else 1, 0)
    pl.semaphore_wait(barrier, peers)

    lane = lax.broadcasted_iota(jnp.int32, (1, 128), 1)
    row8 = lax.broadcasted_iota(jnp.int32, (8, 1), 0)
    table = step_table()

    def step(k, carry):
        inverse = choose(k, [1.0 / math.sqrt(1.0 + r[0] * r[0]) for r in table])
        score_factor = choose(k, [r[1] / r[0] for r in table])
        adjoint_factor = choose(k, [obs_precision * r[1] for r in table])
        noise_factor = choose(k, [r[2] for r in table])

        def remote(index, source, target_ref, b, w):
            return pltpu.make_async_remote_copy(
                src_ref=source, dst_ref=target_ref,
                send_sem=send_sem.at[index], recv_sem=recv_sem.at[k, index],
                device_id={"band": b, "wt": w}, device_id_type=pl.DeviceIdType.MESH,
            )

        copies = [
            (None, remote(0, tsend, tilebuf.at[k, 0], me, right)),
            (None, remote(1, tsend, tilebuf.at[k, 1], me, left)),
            (1, remote(2, sc.at[rows - 1], rowbuf.at[k, 0], me + 1, col)),
            (-1, remote(3, sc.at[0], rowbuf.at[k, 1], me - 1, col)),
            (1, remote(4, tsend, tilebuf.at[k, 2], me + 1, right)),
            (1, remote(5, tsend, tilebuf.at[k, 3], me + 1, left)),
            (-1, remote(6, tsend, tilebuf.at[k, 4], me - 1, right)),
            (-1, remote(7, tsend, tilebuf.at[k, 5], me - 1, left)),
        ]
        parts = [
            (d, remote(8 + i, psend, partbuf.at[k, SPAN - d], me + d, col))
            for i, d in enumerate(dists)
        ]

        def when(d, f):
            if d is None:
                f()
            else:
                pl.when(exists(d))(f)

        tile = jnp.zeros((nv, 128), F32)
        for r in range(rows):
            s = x[pl.ds(r * nv, nv), :] * inverse
            sc[r] = s.astype(BF16)
            tail = pltpu.roll(s[:, lon - 128:], 2 * r + 3, 1)
            start = pltpu.roll(s[:, :128], 2 * r + 1, 1)
            tile = jnp.where(lane == 2 * r + 2, tail, tile)
            tile = jnp.where(lane == 2 * r + 1, start, tile)
        tsend[...] = tile.astype(BF16)
        for d, copy in copies:
            when(d, copy.start)

        high, low = halves(x[...])
        hot = onehot[...]
        picked = nn(high, hot) + nn(low, hot)
        values = jnp.sum(picked * wmask[...], axis=0, keepdims=True)
        high, low = halves(values * offmask[...])
        part = nt(high, slothot[...]) + nt(low, slothot[...])
        psend[...] = jnp.where(row8 == 2 * REACH + 1, sv[...], part)
        for d, copy in parts:
            when(d, copy.start)

        def widen(r, f):
            act[r, 1] = f.astype(BF16)
            near, far = f[:, :128], f[:, lon - 128:]
            a0, a1 = pltpu.roll(near, 1, 1), pltpu.roll(far, 1, 1)
            b0, b1 = pltpu.roll(near, 127, 1), pltpu.roll(far, 127, 1)
            act[r, 0, :, :128] = a0.astype(BF16)
            act[r, 0, :, 128:] = jnp.where(lane == 0, a0, a1).astype(BF16)
            act[r, 2, :, :128] = jnp.where(lane == 127, b1, b0).astype(BF16)
            act[r, 2, :, 128:] = b1.astype(BF16)

        half1 = g1[...]
        wide1 = jnp.concatenate([half1, half1], axis=1)
        for r in range(rows):
            v = nn(lift[...], sc[r])
            lifted[r] = v
            widen(r + 1, silu_rms(v, wide1))

        for d, copy in copies:
            when(None if d is None else -d, copy.wait_recv)
        for r, i in ((0, 0), (rows + 1, 1)):
            widen(r, silu_rms(nn(lift[...], rowbuf[k, i]), wide1))
        t = [tilebuf[k, i].astype(F32) for i in range(6)]
        edge = jnp.where(lane == 0, pltpu.roll(t[2], 128 - 2 * rows, 1), F32(0.0))
        edge = jnp.where(lane == 127, pltpu.roll(t[3], 128 - 2 * rows, 1), edge)
        inner = jnp.logical_and(lane >= 1, lane <= 2 * rows)
        even = lane % 2 == 0
        edge = jnp.where(jnp.logical_and(inner, even), t[0], edge)
        edge = jnp.where(jnp.logical_and(inner, jnp.logical_not(even)), t[1], edge)
        edge = jnp.where(lane == 2 * rows + 2, pltpu.roll(t[4], 2 * rows, 1), edge)
        edge = jnp.where(lane == 2 * rows + 1, pltpu.roll(t[5], 2 * rows, 1), edge)
        rim = silu_rms(nn(lift[...], edge.astype(BF16)), half1)
        for r in range(rows + 2):
            here = rim if r == 0 else pltpu.roll(rim, 128 - 2 * r, 1)
            now = act[r, 0, :, :128].astype(F32)
            act[r, 0, :, :128] = jnp.where(lane == 0, here, now).astype(BF16)
            now = act[r, 2, :, 128:].astype(F32)
            act[r, 2, :, 128:] = jnp.where(lane == 127, here, now).astype(BF16)

        half2 = g2[...]
        wide2 = jnp.concatenate([half2, half2], axis=1)
        scores = []
        for r in range(rows):
            window = act[pl.ds(r, 3)].reshape(9 * nc, lon)
            mixed = lifted[r] + nn(conv[...], window)
            second = silu_rms(mixed, wide2).astype(BF16)
            scores.append(nn(head[...], second))

        for d, copy in parts:
            when(-d, copy.wait_recv)
        mine = psend[...]
        total = mine
        observed = jnp.where(row8 == REACH, sv[...], F32(0.0))
        for d in dists:
            got = partbuf[k, d + SPAN]
            keep = jnp.logical_and(row8 >= max(0, d), row8 <= min(SPAN, SPAN + d))
            total = total + jnp.where(keep, pltpu.roll(got, d % 8, 0), F32(0.0))
            if abs(d) <= REACH:
                observed = jnp.where(row8 == d + REACH, got[SPAN + 1:SPAN + 2], observed)
        difference = jnp.where(row8 <= SPAN, observed - total, F32(0.0))
        innov[...] = difference[REACH:REACH + 1]
        high, low = halves(difference)
        back = nn(high, slothot[...]) + nn(low, slothot[...])
        back = jnp.sum(back * offmask[...], axis=0, keepdims=True)
        high, low = halves(wmask[...] * back)
        adjoint = nt(high, hot) + nt(low, hot)

        for r in range(rows):
            here = pl.ds(r * nv, nv)
            x[here, :] = (
                x[here, :]
                + score_factor * scores[r]
                + adjoint_factor * adjoint[r * nv:(r + 1) * nv]
                + noise_factor * jnp.concatenate(
                    [noise[k, lines_of(r, h), :] for h in range(sides)], axis=1
                )
            )
        for d, copy in copies + parts:
            when(d, copy.wait_send)
        return carry

    lax.fori_loop(0, len(table), step, 0)
    for r in range(rows):
        for h in range(sides):
            out[lines_of(r, h), :] = x[pl.ds(r * nv, nv), 128 * h:128 * (h + 1)]


def per_device(
    nb, nw,
    prior_state, langevin_noise, station_values, entry_cell, entry_owner, entry_slot,
    entry_weight, live_counts, lift_weight, conv_weight, head_weight, first_gain, second_gain,
):
    nv, rows, lon = prior_state.shape
    nc = lift_weight.shape[1]
    steps = langevin_noise.shape[0]
    stations = station_values.shape[0]
    e = entry_cell.shape[0]
    sides = lon // 128
    lines = nv * sides * rows
    x0 = prior_state.reshape(nv, rows, sides, 128).transpose(0, 2, 1, 3).reshape(lines, 128)
    noise = langevin_noise.reshape(steps, nv, rows, sides, 128)
    noise = noise.transpose(0, 1, 3, 2, 4).reshape(steps, lines, 128)
    row = lambda a: a.reshape(1, -1)
    vmem = pl.BlockSpec(memory_space=pltpu.VMEM)
    count = 8 + 2 * SPAN
    state, innov = pl.pallas_call(
        functools.partial(kernel, nb, nw, rows, nv, nc, lon),
        out_shape=(
            jax.ShapeDtypeStruct((lines, 128), F32),
            jax.ShapeDtypeStruct((1, stations), F32),
        ),
        in_specs=[vmem] * 7 + [pl.BlockSpec(memory_space=pltpu.SMEM)] + [vmem] * 5,
        out_specs=(vmem, vmem),
        scratch_shapes=[
            pltpu.VMEM((rows * nv, lon), F32),
            pltpu.VMEM((nc, nv), BF16),
            pltpu.VMEM((nc, 9 * nc), BF16),
            pltpu.VMEM((nc, 128), F32),
            pltpu.VMEM((nc, 128), F32),
            pltpu.VMEM((rows, nv, lon), BF16),
            pltpu.VMEM((rows, nc, lon), F32),
            pltpu.VMEM((rows + 2, 3, nc, lon), BF16),
            pltpu.VMEM((lon, e), BF16),
            pltpu.VMEM((stations, e), BF16),
            pltpu.VMEM((rows * nv, e), F32),
            pltpu.VMEM((8, e), F32),
            pltpu.VMEM((nv, 128), BF16),
            pltpu.VMEM((8, stations), F32),
            pltpu.VMEM((steps, 2, nv, lon), BF16),
            pltpu.VMEM((steps, 6, nv, 128), BF16),
            pltpu.VMEM((steps, 2 * SPAN + 1, 8, stations), F32),
            pltpu.SemaphoreType.DMA((count,)),
            pltpu.SemaphoreType.DMA((steps, count)),
        ],
        compiler_params=pltpu.CompilerParams(
            collective_id=0, has_side_effects=True, vmem_limit_bytes=40 * 1024 * 1024
        ),
    )(
        x0, noise, row(station_values), row(entry_cell), row(entry_owner), row(entry_slot),
        row(entry_weight), live_counts, lift_weight, conv_weight, head_weight.T,
        row(first_gain), row(second_gain),
    )
    state = state.reshape(nv, sides, rows, 128).transpose(0, 2, 1, 3).reshape(nv, rows, lon)
    return state, innov.reshape(-1)


def solution(mesh):
    ring = ("groups", "band", "wt")
    in_specs = (
        P(*ring), P(None, *ring), P(ring), P(ring), P(ring), P(ring), P(ring), P(ring),
        P(), P(), P(), P(), P(),
    )
    out_specs = (P(*ring), P(ring))
    return jax.shard_map(
        functools.partial(per_device, mesh.shape["band"], mesh.shape["wt"]),
        mesh=mesh, in_specs=in_specs, out_specs=out_specs, check_vma=False,
    )
```

```python
import functools
import math

import jax
import jax.numpy as jnp
from jax import lax
from jax.experimental import pallas as pl
from jax.experimental.pallas import tpu as pltpu
from jax.sharding import PartitionSpec as P

REACH = 2
SPAN = 2 * REACH
noise_levels = (1.0, 0.6, 0.3)
obs_precision = 4.0
step_factor = 0.1

F32 = jnp.float32
BF16 = jnp.bfloat16


def step_table():
    rows = []
    for section in range(2):
        upper = noise_levels[section]
        lower = noise_levels[section + 1]
        spread = upper * upper - lower * lower
        rows.append((upper, spread, math.sqrt(spread)))
        factor = step_factor * lower * lower
        rows.append((lower, factor, math.sqrt(2.0 * factor)))
    return rows


def choose(k, values):
    picked = F32(values[-1])
    for i in range(len(values) - 1):
        picked = jnp.where(k == i, F32(values[i]), picked)
    return picked


def nn(a, b):
    return lax.dot_general(a, b, (((1,), (0,)), ((), ())), preferred_element_type=F32)


def nt(a, b):
    return lax.dot_general(a, b, (((1,), (1,)), ((), ())), preferred_element_type=F32)


def halves(a):
    high = a.astype(BF16)
    low = (a - high.astype(F32)).astype(BF16)
    return high, low


def silu_rms(values, half_gain):
    power = jnp.mean(values * values, axis=0, keepdims=True)
    h = values * lax.rsqrt(power + 1e-06) * half_gain
    return h + h * jnp.tanh(h)


CHUNK = 64


def layer(values, half_gain, emit):
    nc, lon = values.shape
    power = jnp.zeros((1, lon), F32)
    for c in range(0, nc, CHUNK):
        v = values[c:c + CHUNK, :]
        power = power + jnp.sum(v * v, axis=0, keepdims=True)
    scale = lax.rsqrt(power * (1.0 / nc) + 1e-06)
    for c in range(0, nc, CHUNK):
        g = half_gain[c:c + CHUNK, :]
        h = values[c:c + CHUNK, :] * scale * jnp.concatenate([g] * (lon // 128), axis=1)
        emit(c, h + h * jnp.tanh(h))


def kernel(nb, nw, rows, nv, nc, lon, *refs):
    inputs, (out, innov) = refs[:13], refs[13:15]
    staged = refs[15:28]
    (
        x, lift, conv, g1, g2, sc, lifted, act, second, onehot, slothot, wmask, offmask,
        tsend, psend, rowbuf, tilebuf, partbuf, send_sem, recv_sem, load_sem,
    ) = refs[28:]
    x0, noise, sv, cell, owner, slot, weight, _, lift_in, conv_in, head, gain1, gain2 = staged
    live = inputs[7]
    loads = [
        pltpu.make_async_copy(source, target, load_sem.at[i])
        for i, (source, target) in enumerate(zip(inputs, staged))
    ]
    for i in (3, 4, 5, 6, 2, 11, 12, 0, 8, 9, 10, 1):
        loads[i].start()
    me = lax.axis_index("band")
    col = lax.axis_index("wt")
    left = lax.rem(col + nw - 1, nw)
    right = lax.rem(col + 1, nw)
    sides = lon // 128

    def lines_of(r, h):
        return pl.ds(h * rows + r, nv, stride=sides * rows)

    dists = [d for d in range(-SPAN, SPAN + 1) if d != 0 and abs(d) < nb]

    def exists(d):
        return jnp.logical_and(me + d >= 0, me + d < nb)

    rowbuf[...] = jnp.zeros_like(rowbuf)
    tilebuf[...] = jnp.zeros_like(tilebuf)
    partbuf[...] = jnp.zeros_like(partbuf)

    barrier = pltpu.get_barrier_semaphore()

    def greet(b, w):
        pl.semaphore_signal(
            barrier, inc=1, device_id={"band": b, "wt": w}, device_id_type=pl.DeviceIdType.MESH
        )

    greet(me, left)
    greet(me, right)
    for d in dists:
        @pl.when(exists(d))
        def _():
            greet(me + d, col)
            if abs(d) == 1:
                greet(me + d, left)
                greet(me + d, right)

    for i in range(13):
        if i not in (1, 7, 9, 10):
            loads[i].wait()
    e = cell.shape[1]
    c = cell[...]
    alive = lax.broadcasted_iota(jnp.int32, (1, e), 1) < live[0]
    weights = jnp.where(alive, weight[...], F32(0.0))
    var = c // (rows * lon)
    rest = c - var * (rows * lon)
    rowof = rest // lon
    lonof = rest - rowof * lon
    target = rowof * nv + var
    first_iota = lax.broadcasted_iota(jnp.int32, (lon, e), 0)
    onehot[...] = jnp.where(first_iota == lonof, F32(1.0), F32(0.0)).astype(BF16)
    slothot[...] = jnp.where(
        lax.broadcasted_iota(jnp.int32, (sv.shape[1], e), 0) == slot[...], F32(1.0), F32(0.0)
    ).astype(BF16)
    wmask[...] = jnp.where(
        lax.broadcasted_iota(jnp.int32, (rows * nv, e), 0) == target, weights, F32(0.0)
    )
    offset = owner[...] - me + REACH
    offmask[...] = jnp.where(
        lax.broadcasted_iota(jnp.int32, (8, e), 0) == offset, F32(1.0), F32(0.0)
    )
    for r in range(rows):
        for h in range(sides):
            x[pl.ds(r * nv, nv), 128 * h:128 * (h + 1)] = x0[lines_of(r, h), :]

    lift[...] = lift_in[...].T
    loads[9].wait()
    for t in range(9):
        conv[:, t * nc:(t + 1) * nc] = conv_in[t].T
    g1[...] = jnp.broadcast_to(0.5 * gain1[...], (128, nc)).T
    g2[...] = jnp.broadcast_to(0.5 * gain2[...], (128, nc)).T

    loads[10].wait()
    loads[1].wait()
    peers = 2
    for d in dists:
        peers = peers + jnp.where(exists(d), 3 if abs(d) == 1 else 1, 0)
    pl.semaphore_wait(barrier, peers)

    lane = lax.broadcasted_iota(jnp.int32, (1, 128), 1)
    row8 = lax.broadcasted_iota(jnp.int32, (8, 1), 0)
    table = step_table()

    def step(k, carry):
        inverse = choose(k, [1.0 / math.sqrt(1.0 + r[0] * r[0]) for r in table])
        score_factor = choose(k, [r[1] / r[0] for r in table])
        adjoint_factor = choose(k, [obs_precision * r[1] for r in table])
        noise_factor = choose(k, [r[2] for r in table])

        def remote(index, source, target_ref, b, w):
            return pltpu.make_async_remote_copy(
                src_ref=source, dst_ref=target_ref,
                send_sem=send_sem.at[index], recv_sem=recv_sem.at[k, index],
                device_id={"band": b, "wt": w}, device_id_type=pl.DeviceIdType.MESH,
            )

        copies = [
            (None, remote(0, tsend, tilebuf.at[k, 0], me, right)),
            (None, remote(1, tsend, tilebuf.at[k, 1], me, left)),
            (1, remote(2, sc.at[rows - 1], rowbuf.at[k, 0], me + 1, col)),
            (-1, remote(3, sc.at[0], rowbuf.at[k, 1], me - 1, col)),
            (1, remote(4, tsend, tilebuf.at[k, 2], me + 1, right)),
            (1, remote(5, tsend, tilebuf.at[k, 3], me + 1, left)),
            (-1, remote(6, tsend, tilebuf.at[k, 4], me - 1, right)),
            (-1, remote(7, tsend, tilebuf.at[k, 5], me - 1, left)),
        ]
        parts = [
            (d, remote(8 + i, psend, partbuf.at[k, SPAN - d], me + d, col))
            for i, d in enumerate(dists)
        ]

        def when(d, f):
            if d is None:
                f()
            else:
                pl.when(exists(d))(f)

        tile = jnp.zeros((nv, 128), F32)
        for r in range(rows):
            s = x[pl.ds(r * nv, nv), :] * inverse
            sc[r] = s.astype(BF16)
            tail = pltpu.roll(s[:, lon - 128:], 2 * r + 3, 1)
            start = pltpu.roll(s[:, :128], 2 * r + 1, 1)
            tile = jnp.where(lane == 2 * r + 2, tail, tile)
            tile = jnp.where(lane == 2 * r + 1, start, tile)
        tsend[...] = tile.astype(BF16)
        for d, copy in copies:
            when(d, copy.start)

        high, low = halves(x[...])
        hot = onehot[...]
        picked = nn(high, hot) + nn(low, hot)
        values = jnp.sum(picked * wmask[...], axis=0, keepdims=True)
        high, low = halves(values * offmask[...])
        part = nt(high, slothot[...]) + nt(low, slothot[...])
        psend[...] = jnp.where(row8 == 2 * REACH + 1, sv[...], part)

        def widen(r, source, slot):
            lifted[slot] = nn(lift[...], source)

            def emit(c, f):
                part = slice(c, c + CHUNK)
                act[r, 1, part, :] = f.astype(BF16)
                near, far = f[:, :128], f[:, lon - 128:]
                a0, a1 = pltpu.roll(near, 1, 1), pltpu.roll(far, 1, 1)
                b0, b1 = pltpu.roll(near, 127, 1), pltpu.roll(far, 127, 1)
                act[r, 0, part, :128] = a0.astype(BF16)
                act[r, 0, part, 128:] = jnp.where(lane == 0, a0, a1).astype(BF16)
                act[r, 2, part, :128] = jnp.where(lane == 127, b1, b0).astype(BF16)
                act[r, 2, part, 128:] = b1.astype(BF16)

            layer(lifted.at[slot], g1, emit)

        def patch(edge, which):
            rim = silu_rms(nn(lift[...], edge.astype(BF16)), g1[...])
            for r in which:
                here = rim if r == 0 else pltpu.roll(rim, 128 - 2 * r, 1)
                now = act[r, 0, :, :128].astype(F32)
                act[r, 0, :, :128] = jnp.where(lane == 0, here, now).astype(BF16)
                now = act[r, 2, :, 128:].astype(F32)
                act[r, 2, :, 128:] = jnp.where(lane == 127, here, now).astype(BF16)

        def convolve(r):
            window = act[pl.ds(r, 3)].reshape(9 * nc, lon)
            lifted[r] = lifted[r] + nn(conv[...], window)

            def emit(c, f):
                second[r, c:c + CHUNK, :] = f.astype(BF16)

            layer(lifted.at[r], g2, emit)

        widen(1, sc[0], 0)
        for d, copy in parts:
            when(d, copy.start)
        for r in range(1, rows):
            widen(r + 1, sc[r], r)

        for d, copy in copies[:2]:
            copy.wait_recv()
        even = lane % 2 == 0
        inner = jnp.logical_and(lane >= 1, lane <= 2 * rows)
        edge = jnp.where(even, tilebuf[k, 0].astype(F32), tilebuf[k, 1].astype(F32))
        patch(jnp.where(inner, edge, F32(0.0)), range(1, rows + 1))
        for r in range(1, rows - 1):
            convolve(r)

        for d, copy in copies[2:]:
            when(-d, copy.wait_recv)
        for r, i in ((0, 0), (rows + 1, 1)):
            widen(r, rowbuf[k, i], rows + i)
        t = [tilebuf[k, i].astype(F32) for i in range(2, 6)]
        edge = jnp.where(lane == 0, pltpu.roll(t[0], 128 - 2 * rows, 1), F32(0.0))
        edge = jnp.where(lane == 127, pltpu.roll(t[1], 128 - 2 * rows, 1), edge)
        edge = jnp.where(lane == 2 * rows + 2, pltpu.roll(t[2], 2 * rows, 1), edge)
        edge = jnp.where(lane == 2 * rows + 1, pltpu.roll(t[3], 2 * rows, 1), edge)
        patch(edge, (0, rows + 1))
        convolve(0)

        for d, copy in parts:
            when(-d, copy.wait_recv)
        convolve(rows - 1)
        total = psend[...]
        observed = jnp.where(row8 == REACH, sv[...], F32(0.0))
        for d in dists:
            got = partbuf[k, d + SPAN]
            keep = jnp.logical_and(row8 >= max(0, d), row8 <= min(SPAN, SPAN + d))
            total = total + jnp.where(keep, pltpu.roll(got, d % 8, 0), F32(0.0))
            if abs(d) <= REACH:
                observed = jnp.where(row8 == d + REACH, got[SPAN + 1:SPAN + 2], observed)
        difference = jnp.where(row8 <= SPAN, observed - total, F32(0.0))
        innov[...] = difference[REACH:REACH + 1]
        high, low = halves(difference)
        back = nn(high, slothot[...]) + nn(low, slothot[...])
        back = jnp.sum(back * offmask[...], axis=0, keepdims=True)
        high, low = halves(wmask[...] * back)
        adjoint = nt(high, onehot[...]) + nt(low, onehot[...])
        scores = [nn(head[...], second[r]) for r in range(rows)]

        for r in range(rows):
            here = pl.ds(r * nv, nv)
            x[here, :] = (
                x[here, :]
                + score_factor * scores[r]
                + adjoint_factor * adjoint[r * nv:(r + 1) * nv]
                + noise_factor * jnp.concatenate(
                    [noise[k, lines_of(r, h), :] for h in range(sides)], axis=1
                )
            )
        for d, copy in copies + parts:
            when(d, copy.wait_send)
        return carry

    lax.fori_loop(0, len(table), step, 0)
    for r in range(rows):
        for h in range(sides):
            out[lines_of(r, h), :] = x[pl.ds(r * nv, nv), 128 * h:128 * (h + 1)]


def per_device(
    nb, nw,
    prior_state, langevin_noise, station_values, entry_cell, entry_owner, entry_slot,
    entry_weight, live_counts, lift_weight, conv_weight, head_weight, first_gain, second_gain,
):
    nv, rows, lon = prior_state.shape
    nc = lift_weight.shape[1]
    steps = langevin_noise.shape[0]
    stations = station_values.shape[0]
    e = entry_cell.shape[0]
    sides = lon // 128
    lines = nv * sides * rows
    x0 = prior_state.reshape(nv, rows, sides, 128).transpose(0, 2, 1, 3).reshape(lines, 128)
    noise = langevin_noise.reshape(steps, nv, rows, sides, 128)
    noise = noise.transpose(0, 1, 3, 2, 4).reshape(steps, lines, 128)
    row = lambda a: a.reshape(1, -1)
    vmem = pl.BlockSpec(memory_space=pltpu.VMEM)
    count = 8 + 2 * SPAN
    operands = (
        x0, noise, row(station_values), row(entry_cell), row(entry_owner), row(entry_slot),
        row(entry_weight), live_counts, lift_weight, conv_weight, head_weight.T,
        row(first_gain), row(second_gain),
    )
    space = lambda i: pltpu.SMEM if i == 7 else pltpu.VMEM
    state, innov = pl.pallas_call(
        functools.partial(kernel, nb, nw, rows, nv, nc, lon),
        out_shape=(
            jax.ShapeDtypeStruct((lines, 128), F32),
            jax.ShapeDtypeStruct((1, stations), F32),
        ),
        in_specs=[
            pl.BlockSpec(memory_space=pltpu.SMEM if i == 7 else pl.ANY)
            for i in range(len(operands))
        ],
        out_specs=(vmem, vmem),
        scratch_shapes=[space(i)(a.shape, a.dtype) for i, a in enumerate(operands)] + [
            pltpu.VMEM((rows * nv, lon), F32),
            pltpu.VMEM((nc, nv), BF16),
            pltpu.VMEM((nc, 9 * nc), BF16),
            pltpu.VMEM((nc, 128), F32),
            pltpu.VMEM((nc, 128), F32),
            pltpu.VMEM((rows, nv, lon), BF16),
            pltpu.VMEM((rows + 2, nc, lon), F32),
            pltpu.VMEM((rows + 2, 3, nc, lon), BF16),
            pltpu.VMEM((rows, nc, lon), BF16),
            pltpu.VMEM((lon, e), BF16),
            pltpu.VMEM((stations, e), BF16),
            pltpu.VMEM((rows * nv, e), F32),
            pltpu.VMEM((8, e), F32),
            pltpu.VMEM((nv, 128), BF16),
            pltpu.VMEM((8, stations), F32),
            pltpu.VMEM((steps, 2, nv, lon), BF16),
            pltpu.VMEM((steps, 6, nv, 128), BF16),
            pltpu.VMEM((steps, 2 * SPAN + 1, 8, stations), F32),
            pltpu.SemaphoreType.DMA((count,)),
            pltpu.SemaphoreType.DMA((steps, count)),
            pltpu.SemaphoreType.DMA((len(operands),)),
        ],
        compiler_params=pltpu.CompilerParams(
            collective_id=0, has_side_effects=True, vmem_limit_bytes=40 * 1024 * 1024
        ),
    )(*operands)
    state = state.reshape(nv, sides, rows, 128).transpose(0, 2, 1, 3).reshape(nv, rows, lon)
    return state, innov.reshape(-1)


def solution(mesh):
    ring = ("groups", "band", "wt")
    in_specs = (
        P(*ring), P(None, *ring), P(ring), P(ring), P(ring), P(ring), P(ring), P(ring),
        P(), P(), P(), P(), P(),
    )
    out_specs = (P(*ring), P(ring))
    return jax.shard_map(
        functools.partial(per_device, mesh.shape["band"], mesh.shape["wt"]),
        mesh=mesh, in_specs=in_specs, out_specs=out_specs, check_vma=False,
    )
```

```python
import functools
import math

import jax
import jax.numpy as jnp
from jax import lax
from jax.experimental import pallas as pl
from jax.experimental.pallas import tpu as pltpu
from jax.sharding import PartitionSpec as P

REACH = 2
SPAN = 2 * REACH
noise_levels = (1.0, 0.6, 0.3)
obs_precision = 4.0
step_factor = 0.1

F32 = jnp.float32
BF16 = jnp.bfloat16


def step_table():
    rows = []
    for section in range(2):
        upper = noise_levels[section]
        lower = noise_levels[section + 1]
        spread = upper * upper - lower * lower
        rows.append((upper, spread, math.sqrt(spread)))
        factor = step_factor * lower * lower
        rows.append((lower, factor, math.sqrt(2.0 * factor)))
    return rows


def choose(k, values):
    picked = F32(values[-1])
    for i in range(len(values) - 1):
        picked = jnp.where(k == i, F32(values[i]), picked)
    return picked


def nn(a, b):
    return lax.dot_general(a, b, (((1,), (0,)), ((), ())), preferred_element_type=F32)


def nt(a, b):
    return lax.dot_general(a, b, (((1,), (1,)), ((), ())), preferred_element_type=F32)


def halves(a):
    high = a.astype(BF16)
    low = (a - high.astype(F32)).astype(BF16)
    return high, low


def silu_rms(values, half_gain):
    power = jnp.mean(values * values, axis=0, keepdims=True)
    h = values * lax.rsqrt(power + 1e-06) * half_gain
    return h + h * jnp.tanh(h)


CHUNK = 64


def layer(values, half_gain, emit):
    nc, lon = values.shape
    power = jnp.zeros((1, lon), F32)
    for c in range(0, nc, CHUNK):
        v = values[c:c + CHUNK, :]
        power = power + jnp.sum(v * v, axis=0, keepdims=True)
    scale = lax.rsqrt(power * (1.0 / nc) + 1e-06)
    for c in range(0, nc, CHUNK):
        g = half_gain[c:c + CHUNK, :]
        h = values[c:c + CHUNK, :] * scale * jnp.concatenate([g] * (lon // 128), axis=1)
        emit(c, h + h * jnp.tanh(h))


def kernel(nb, nw, rows, nv, nc, lon, *refs):
    inputs, (out, innov) = refs[:13], refs[13:15]
    staged = refs[15:28]
    (
        x, lift, conv, g1, g2, sc, lifted, act, second, onehot, slothot, wmask, offmask,
        tsend, psend, rowbuf, tilebuf, partbuf, send_sem, recv_sem, load_sem,
    ) = refs[28:]
    x0, noise, sv, cell, owner, slot, weight, _, lift_in, conv_in, head, gain1, gain2 = staged
    live = inputs[7]
    loads = {
        i: pltpu.make_async_copy(inputs[i], staged[i], load_sem.at[i])
        for i in range(len(inputs)) if i != 7
    }
    for i in (3, 4, 5, 6, 2, 11, 12, 0, 8, 9, 10, 1):
        loads[i].start()
    me = lax.axis_index("band")
    col = lax.axis_index("wt")
    left = lax.rem(col + nw - 1, nw)
    right = lax.rem(col + 1, nw)
    sides = lon // 128

    def lines_of(r, h):
        return pl.ds(h * rows + r, nv, stride=sides * rows)

    dists = [d for d in range(-SPAN, SPAN + 1) if d != 0 and abs(d) < nb]

    def exists(d):
        return jnp.logical_and(me + d >= 0, me + d < nb)

    rowbuf[...] = jnp.zeros_like(rowbuf)
    tilebuf[...] = jnp.zeros_like(tilebuf)
    partbuf[...] = jnp.zeros_like(partbuf)

    barrier = pltpu.get_barrier_semaphore()

    def greet(b, w):
        pl.semaphore_signal(
            barrier, inc=1, device_id={"band": b, "wt": w}, device_id_type=pl.DeviceIdType.MESH
        )

    greet(me, left)
    greet(me, right)
    for d in dists:
        @pl.when(exists(d))
        def _():
            greet(me + d, col)
            if abs(d) == 1:
                greet(me + d, left)
                greet(me + d, right)

    for i in range(13):
        if i not in (1, 7, 9, 10):
            loads[i].wait()
    e = cell.shape[1]
    c = cell[...]
    alive = lax.broadcasted_iota(jnp.int32, (1, e), 1) < live[0]
    weights = jnp.where(alive, weight[...], F32(0.0))
    var = c // (rows * lon)
    rest = c - var * (rows * lon)
    rowof = rest // lon
    lonof = rest - rowof * lon
    target = rowof * nv + var
    first_iota = lax.broadcasted_iota(jnp.int32, (lon, e), 0)
    onehot[...] = jnp.where(first_iota == lonof, F32(1.0), F32(0.0)).astype(BF16)
    slothot[...] = jnp.where(
        lax.broadcasted_iota(jnp.int32, (sv.shape[1], e), 0) == slot[...], F32(1.0), F32(0.0)
    ).astype(BF16)
    wmask[...] = jnp.where(
        lax.broadcasted_iota(jnp.int32, (rows * nv, e), 0) == target, weights, F32(0.0)
    )
    offset = owner[...] - me + REACH
    offmask[...] = jnp.where(
        lax.broadcasted_iota(jnp.int32, (8, e), 0) == offset, F32(1.0), F32(0.0)
    )
    for r in range(rows):
        for h in range(sides):
            x[pl.ds(r * nv, nv), 128 * h:128 * (h + 1)] = x0[lines_of(r, h), :]

    lift[...] = lift_in[...].T
    loads[9].wait()
    for t in range(9):
        conv[:, t * nc:(t + 1) * nc] = conv_in[t].T
    g1[...] = jnp.broadcast_to(0.5 * gain1[...], (128, nc)).T
    g2[...] = jnp.broadcast_to(0.5 * gain2[...], (128, nc)).T

    loads[10].wait()
    loads[1].wait()
    peers = 2
    for d in dists:
        peers = peers + jnp.where(exists(d), 3 if abs(d) == 1 else 1, 0)
    pl.semaphore_wait(barrier, peers)

    lane = lax.broadcasted_iota(jnp.int32, (1, 128), 1)
    row8 = lax.broadcasted_iota(jnp.int32, (8, 1), 0)
    table = step_table()

    def step(k, carry):
        inverse = choose(k, [1.0 / math.sqrt(1.0 + r[0] * r[0]) for r in table])
        score_factor = choose(k, [r[1] / r[0] for r in table])
        adjoint_factor = choose(k, [obs_precision * r[1] for r in table])
        noise_factor = choose(k, [r[2] for r in table])

        def remote(index, source, target_ref, b, w):
            return pltpu.make_async_remote_copy(
                src_ref=source, dst_ref=target_ref,
                send_sem=send_sem.at[index], recv_sem=recv_sem.at[k, index],
                device_id={"band": b, "wt": w}, device_id_type=pl.DeviceIdType.MESH,
            )

        copies = [
            (None, remote(0, tsend, tilebuf.at[k, 0], me, right)),
            (None, remote(1, tsend, tilebuf.at[k, 1], me, left)),
            (1, remote(2, sc.at[rows - 1], rowbuf.at[k, 0], me + 1, col)),
            (-1, remote(3, sc.at[0], rowbuf.at[k, 1], me - 1, col)),
            (1, remote(4, tsend, tilebuf.at[k, 2], me + 1, right)),
            (1, remote(5, tsend, tilebuf.at[k, 3], me + 1, left)),
            (-1, remote(6, tsend, tilebuf.at[k, 4], me - 1, right)),
            (-1, remote(7, tsend, tilebuf.at[k, 5], me - 1, left)),
        ]
        parts = [
            (d, remote(8 + i, psend, partbuf.at[k, SPAN - d], me + d, col))
            for i, d in enumerate(dists)
        ]

        def when(d, f):
            if d is None:
                f()
            else:
                pl.when(exists(d))(f)

        tile = jnp.zeros((nv, 128), F32)
        for r in range(rows):
            s = x[pl.ds(r * nv, nv), :] * inverse
            sc[r] = s.astype(BF16)
            tail = pltpu.roll(s[:, lon - 128:], 2 * r + 3, 1)
            start = pltpu.roll(s[:, :128], 2 * r + 1, 1)
            tile = jnp.where(lane == 2 * r + 2, tail, tile)
            tile = jnp.where(lane == 2 * r + 1, start, tile)
        tsend[...] = tile.astype(BF16)
        for d, copy in copies:
            when(d, copy.start)

        high, low = halves(x[...])
        hot = onehot[...]
        picked = nn(high, hot) + nn(low, hot)
        values = jnp.sum(picked * wmask[...], axis=0, keepdims=True)
        high, low = halves(values * offmask[...])
        part = nt(high, slothot[...]) + nt(low, slothot[...])
        psend[...] = jnp.where(row8 == 2 * REACH + 1, sv[...], part)

        def widen(r, source, slot):
            lifted[slot] = nn(lift[...], source)

            def emit(c, f):
                part = slice(c, c + CHUNK)
                act[r, 1, part, :] = f.astype(BF16)
                near, far = f[:, :128], f[:, lon - 128:]
                a0, a1 = pltpu.roll(near, 1, 1), pltpu.roll(far, 1, 1)
                b0, b1 = pltpu.roll(near, 127, 1), pltpu.roll(far, 127, 1)
                act[r, 0, part, :128] = a0.astype(BF16)
                act[r, 0, part, 128:] = jnp.where(lane == 0, a0, a1).astype(BF16)
                act[r, 2, part, :128] = jnp.where(lane == 127, b1, b0).astype(BF16)
                act[r, 2, part, 128:] = b1.astype(BF16)

            layer(lifted.at[slot], g1, emit)

        def patch(edge, which):
            rim = silu_rms(nn(lift[...], edge.astype(BF16)), g1[...])
            for r in which:
                here = rim if r == 0 else pltpu.roll(rim, 128 - 2 * r, 1)
                now = act[r, 0, :, :128].astype(F32)
                act[r, 0, :, :128] = jnp.where(lane == 0, here, now).astype(BF16)
                now = act[r, 2, :, 128:].astype(F32)
                act[r, 2, :, 128:] = jnp.where(lane == 127, here, now).astype(BF16)

        def convolve(r):
            window = act[pl.ds(r, 3)].reshape(9 * nc, lon)
            lifted[r] = lifted[r] + nn(conv[...], window)

            def emit(c, f):
                second[r, c:c + CHUNK, :] = f.astype(BF16)

            layer(lifted.at[r], g2, emit)

        widen(1, sc[0], 0)
        for d, copy in parts:
            when(d, copy.start)
        for r in range(1, rows):
            widen(r + 1, sc[r], r)

        for d, copy in copies[:2]:
            copy.wait_recv()
        even = lane % 2 == 0
        inner = jnp.logical_and(lane >= 1, lane <= 2 * rows)
        edge = jnp.where(even, tilebuf[k, 0].astype(F32), tilebuf[k, 1].astype(F32))
        patch(jnp.where(inner, edge, F32(0.0)), range(1, rows + 1))
        for r in range(1, rows - 1):
            convolve(r)

        for d, copy in copies[2:]:
            when(-d, copy.wait_recv)
        for r, i in ((0, 0), (rows + 1, 1)):
            widen(r, rowbuf[k, i], rows + i)
        t = [tilebuf[k, i].astype(F32) for i in range(2, 6)]
        edge = jnp.where(lane == 0, pltpu.roll(t[0], 128 - 2 * rows, 1), F32(0.0))
        edge = jnp.where(lane == 127, pltpu.roll(t[1], 128 - 2 * rows, 1), edge)
        edge = jnp.where(lane == 2 * rows + 2, pltpu.roll(t[2], 2 * rows, 1), edge)
        edge = jnp.where(lane == 2 * rows + 1, pltpu.roll(t[3], 2 * rows, 1), edge)
        patch(edge, (0, rows + 1))
        convolve(0)

        for d, copy in parts:
            when(-d, copy.wait_recv)
        convolve(rows - 1)
        total = psend[...]
        observed = jnp.where(row8 == REACH, sv[...], F32(0.0))
        for d in dists:
            got = partbuf[k, d + SPAN]
            keep = jnp.logical_and(row8 >= max(0, d), row8 <= min(SPAN, SPAN + d))
            total = total + jnp.where(keep, pltpu.roll(got, d % 8, 0), F32(0.0))
            if abs(d) <= REACH:
                observed = jnp.where(row8 == d + REACH, got[SPAN + 1:SPAN + 2], observed)
        difference = jnp.where(row8 <= SPAN, observed - total, F32(0.0))
        innov[...] = difference[REACH:REACH + 1]
        high, low = halves(difference)
        back = nn(high, slothot[...]) + nn(low, slothot[...])
        back = jnp.sum(back * offmask[...], axis=0, keepdims=True)
        high, low = halves(wmask[...] * back)
        adjoint = nt(high, onehot[...]) + nt(low, onehot[...])
        scores = [nn(head[...], second[r]) for r in range(rows)]

        for r in range(rows):
            here = pl.ds(r * nv, nv)
            x[here, :] = (
                x[here, :]
                + score_factor * scores[r]
                + adjoint_factor * adjoint[r * nv:(r + 1) * nv]
                + noise_factor * jnp.concatenate(
                    [noise[k, lines_of(r, h), :] for h in range(sides)], axis=1
                )
            )
        for d, copy in copies + parts:
            when(d, copy.wait_send)
        return carry

    lax.fori_loop(0, len(table), step, 0)
    for r in range(rows):
        for h in range(sides):
            out[lines_of(r, h), :] = x[pl.ds(r * nv, nv), 128 * h:128 * (h + 1)]


def per_device(
    nb, nw,
    prior_state, langevin_noise, station_values, entry_cell, entry_owner, entry_slot,
    entry_weight, live_counts, lift_weight, conv_weight, head_weight, first_gain, second_gain,
):
    nv, rows, lon = prior_state.shape
    nc = lift_weight.shape[1]
    steps = langevin_noise.shape[0]
    stations = station_values.shape[0]
    e = entry_cell.shape[0]
    sides = lon // 128
    lines = nv * sides * rows
    x0 = prior_state.reshape(nv, rows, sides, 128).transpose(0, 2, 1, 3).reshape(lines, 128)
    noise = langevin_noise.reshape(steps, nv, rows, sides, 128)
    noise = noise.transpose(0, 1, 3, 2, 4).reshape(steps, lines, 128)
    row = lambda a: a.reshape(1, -1)
    vmem = pl.BlockSpec(memory_space=pltpu.VMEM)
    count = 8 + 2 * SPAN
    operands = (
        x0, noise, row(station_values), row(entry_cell), row(entry_owner), row(entry_slot),
        row(entry_weight), live_counts, lift_weight, conv_weight, head_weight.T,
        row(first_gain), row(second_gain),
    )
    space = lambda i: pltpu.SMEM if i == 7 else pltpu.VMEM
    state, innov = pl.pallas_call(
        functools.partial(kernel, nb, nw, rows, nv, nc, lon),
        out_shape=(
            jax.ShapeDtypeStruct((lines, 128), F32),
            jax.ShapeDtypeStruct((1, stations), F32),
        ),
        in_specs=[
            pl.BlockSpec(memory_space=pltpu.SMEM if i == 7 else pltpu.HBM)
            for i in range(len(operands))
        ],
        out_specs=(vmem, vmem),
        scratch_shapes=[space(i)(a.shape, a.dtype) for i, a in enumerate(operands)] + [
            pltpu.VMEM((rows * nv, lon), F32),
            pltpu.VMEM((nc, nv), BF16),
            pltpu.VMEM((nc, 9 * nc), BF16),
            pltpu.VMEM((nc, 128), F32),
            pltpu.VMEM((nc, 128), F32),
            pltpu.VMEM((rows, nv, lon), BF16),
            pltpu.VMEM((rows + 2, nc, lon), F32),
            pltpu.VMEM((rows + 2, 3, nc, lon), BF16),
            pltpu.VMEM((rows, nc, lon), BF16),
            pltpu.VMEM((lon, e), BF16),
            pltpu.VMEM((stations, e), BF16),
            pltpu.VMEM((rows * nv, e), F32),
            pltpu.VMEM((8, e), F32),
            pltpu.VMEM((nv, 128), BF16),
            pltpu.VMEM((8, stations), F32),
            pltpu.VMEM((steps, 2, nv, lon), BF16),
            pltpu.VMEM((steps, 6, nv, 128), BF16),
            pltpu.VMEM((steps, 2 * SPAN + 1, 8, stations), F32),
            pltpu.SemaphoreType.DMA((count,)),
            pltpu.SemaphoreType.DMA((steps, count)),
            pltpu.SemaphoreType.DMA((len(operands),)),
        ],
        compiler_params=pltpu.CompilerParams(
            collective_id=0, has_side_effects=True, vmem_limit_bytes=58 * 1024 * 1024
        ),
    )(*operands)
    state = state.reshape(nv, sides, rows, 128).transpose(0, 2, 1, 3).reshape(nv, rows, lon)
    return state, innov.reshape(-1)


def solution(mesh):
    ring = ("groups", "band", "wt")
    in_specs = (
        P(*ring), P(None, *ring), P(ring), P(ring), P(ring), P(ring), P(ring), P(ring),
        P(), P(), P(), P(), P(),
    )
    out_specs = (P(*ring), P(ring))
    return jax.shard_map(
        functools.partial(per_device, mesh.shape["band"], mesh.shape["wt"]),
        mesh=mesh, in_specs=in_specs, out_specs=out_specs, check_vma=False,
    )
```
